512 devices in a mesh: occ: 8 (over z), vir: 64 (over y, x, core).
Axes of the slice: x: 4, y: 8, z: 8, core: 2. Of those that a mesh axis runs over, the one named last changes fastest.
Arguments:
- amplitudes: bfloat16 [6144, 2048], P('occ', 'vir'), may hold values from -6 to 6
- integrals: bfloat16 [2048, 163840], P('occ', 'vir'), may hold values from -0.375 to 0.375
- occ_sym: int32 [48], P('occ'), may hold values from 0 to 7, as said below
- vir_sym: int32 [1280], P('vir'), may hold values from 0 to 7, as said below
- k_sym: int32 [16], replicated, may hold values from 0 to 7
Outputs:
- ladder: bfloat16 [6144, 163840], P('occ', 'vir')
The draws below stay inside these ranges and needn't reach their ends.
Inputs may be any that keep to these rules, and one draw needn't show every extreme that they name: `occ_sym`: among the 6 blocks of one index of occ no irrep occurs more than 2 times, and one occurs exactly 2 times. `vir_sym`: among the 20 blocks of one index of vir no irrep occurs more than 5 times, and one occurs exactly 5 times.
All inputs are finite; a program needn't handle non-finite values.
Results may differ from the reference program's by a relative error of at most 0.001.
Values may be sent and summed in bfloat16 or wider, within the bound.
A program may use at most 64 MiB of HBM per device.

```python
import jax
import jax.numpy as jnp
from jax import lax

BLK = 128
IRREPS = 8
OCC_DEV = 768
VB_DEV = 20
KB = 16
MAXO = 2
MAXB = 5
OCC_PAIRS = 6144
VBLOCKS = 1280
VPAIRS = 163840
KWIN = 2048
N_VIR = 64


def skewed_irreps(key, groups, group_size, slot_bound):
    group_keys = jax.random.split(key, groups)

    def per_group(group_key):
        first_key, second_key, third_key = jax.random.split(group_key, 3)
        hottest = jax.random.randint(first_key, (), 0, IRREPS)
        offset = jax.random.randint(second_key, (), 0, IRREPS - 1)
        places = jnp.arange(group_size, dtype=jnp.int32)
        others = (hottest + 1 + (offset + places - slot_bound) % (IRREPS - 1)) % IRREPS
        labels = jnp.where(places < slot_bound, hottest, others).astype(jnp.int32)
        return jax.random.permutation(third_key, labels)
    return jax.vmap(per_group)(group_keys).reshape(groups * group_size)


def draw_occ_sym(key, part):
    return skewed_irreps(key, OCC_PAIRS // OCC_DEV, OCC_DEV // BLK, MAXO)


def draw_vir_sym(key, part):
    return skewed_irreps(key, VBLOCKS // VB_DEV, VB_DEV, MAXB)


def touch_ends(values, own_key, low, top_value):
    longest = values.shape.index(max(values.shape))
    spots = []
    for shift in (0, 1):
        where = [jax.random.randint(jax.random.fold_in(own_key, axis), (), 0, length) for axis, length in enumerate(values.shape)]
        where[longest] = (where[longest] + shift) % values.shape[longest]
        spots.append(tuple(where))
    return values.at[spots[0]].set(low).at[spots[1]].set(top_value)


def shard_levels(key, shape, shards, smallest, high):
    gain, own = 1.0, jax.random.fold_in(key, 6)
    for dim, shards_of in shards:
        steps = jnp.exp(jax.random.uniform(jax.random.fold_in(own, dim), (shards_of,), jnp.float32, smallest / len(shards), high / len(shards)))
        gain = gain * jnp.repeat(steps, shape[dim] // shards_of).reshape([-1 if axis == dim else 1 for axis in range(len(shape))])
    return gain


def gaussian(own_key, dims, deviation, bound, cuts=(), kind=jnp.bfloat16):
    loudness = shard_levels(own_key, dims, cuts, -0.22, 0.18) if cuts else 1.0
    array = jax.random.normal(own_key, dims, jnp.float32) * deviation * loudness
    return jnp.minimum(jnp.maximum(array, -bound), bound).astype(kind)


def setup_inputs(seed: int = 0) -> dict:
    seeds = jax.random.split(jax.random.key(seed), 6)
    amplitudes = gaussian(seeds[0], (OCC_PAIRS, KWIN), 1.0, 6.0, ((0, 8), (1, 64)))
    integrals = gaussian(seeds[1], (KWIN, VPAIRS), (2 * BLK) ** -0.5, 0.375, ((0, 8), (1, 64)))
    occ_sym = draw_occ_sym(jax.random.fold_in(seeds[5], 71), 0)
    vir_sym = draw_vir_sym(jax.random.fold_in(seeds[5], 71), 0)
    k_sym = touch_ends(jax.random.randint(seeds[4], (KB,), 0, IRREPS), jax.random.fold_in(seeds[4], 1), 0, IRREPS - 1).astype(jnp.int32)
    return dict(amplitudes=amplitudes, integrals=integrals, occ_sym=occ_sym, vir_sym=vir_sym, k_sym=k_sym)


def slot_order(symmetry, labels, slot_bound):
    label_count = labels.shape[0]
    positions = jnp.arange(label_count, dtype=jnp.int32)
    matching = labels == symmetry
    ranking = jnp.where(matching, positions, positions + label_count)
    chosen = jnp.argsort(ranking)[:slot_bound].astype(jnp.int32)
    return chosen, matching[chosen]


def reference(amplitudes, integrals, occ_sym, vir_sym, k_sym):
    occ_blocks = occ_sym.shape[0]
    kblocks = k_sym.shape[0]
    allowed = (occ_sym[:, None] == k_sym[None, :]).astype(amplitudes.dtype)
    amp_masked = (amplitudes.reshape(occ_blocks, BLK, kblocks, BLK) * allowed[:, None, :, None]).reshape(OCC_PAIRS, KWIN)

    def one_span(device):
        device = device.astype(jnp.int32)
        labels = lax.dynamic_slice_in_dim(vir_sym, device * VB_DEV, VB_DEV)
        columns = lax.dynamic_slice_in_dim(integrals, device * (VB_DEV * BLK), VB_DEV * BLK, 1).reshape(KWIN, VB_DEV, BLK)

        def per_block(block_index, running):
            block_index = block_index.astype(jnp.int32)
            symmetry = k_sym[block_index]
            chosen, usable = slot_order(symmetry, labels, MAXB)
            block_rows = lax.dynamic_slice_in_dim(columns, block_index * BLK, BLK, 0)
            packed = block_rows[:, chosen, :] * usable[None, :, None].astype(block_rows.dtype)
            amp_cols = lax.dynamic_slice_in_dim(amp_masked, block_index * BLK, BLK, 1)
            product = jnp.dot(amp_cols, packed.reshape(BLK, MAXB * BLK), preferred_element_type=jnp.float32)
            return running.at[:, chosen, :].add(product.reshape(OCC_PAIRS, MAXB, BLK))

        summed = lax.fori_loop(0, kblocks, per_block, jnp.zeros((OCC_PAIRS, VB_DEV, BLK), jnp.float32))
        return summed.reshape(OCC_PAIRS, VB_DEV * BLK).astype(jnp.bfloat16)

    def fill(device, result):
        device = jnp.asarray(device).astype(jnp.int32)
        return lax.dynamic_update_slice_in_dim(result, one_span(device), device * (VB_DEV * BLK), 1)

    return lax.fori_loop(0, N_VIR, fill, jnp.zeros((OCC_PAIRS, VPAIRS), jnp.bfloat16))
```

```python
import jax
import jax.numpy as jnp
from jax import lax
from jax.experimental import pallas as pl
from jax.experimental.pallas import tpu as pltpu
from jax.sharding import PartitionSpec as P

BLK = 128
MAXO = 2
MAXB = 5
NZ, NY, NX = 8, 8, 4
PIECES = 4
MESH = pl.DeviceIdType.MESH


def ladder_kernel(occ_s, vir_s, k_s, a_hbm, v_hbm, out_ref, a_in, v_in, ag, vbuf, amask, acc,
                  in_sem, vsend, vrecv, xsend, xrecv, ysend, yrecv, csend, crecv):
    occ_rows = out_ref.shape[0]
    occ_blocks = occ_rows // BLK
    vir_blocks = vir_s.shape[0]
    width = MAXB * BLK
    z = lax.axis_index("occ")
    v = lax.axis_index("vir")
    y = lax.div(v, 2 * NX)
    x = lax.rem(lax.div(v, 2), NX)
    c = lax.rem(v, 2)

    def vir_at(yy, xx, cc):
        return (yy * NX + xx) * 2 + cc

    def ring(value, step, size):
        return lax.rem(value + step + size, size)

    z_next, z_prev = (ring(z, 1, NZ), v), (ring(z, -1, NZ), v)
    y_next, y_prev = (z, vir_at(ring(y, 1, NY), x, c)), (z, vir_at(ring(y, -1, NY), x, c))
    x_far = {step: (z, vir_at(y, ring(x, step, NX), c)) for step in (1, 3, 2)}
    twin = (z, vir_at(y, x, 1 - c))
    partners = [z_next, z_prev, y_next, y_prev, twin] + list(x_far.values())

    barrier = pltpu.get_barrier_semaphore()
    for partner in partners:
        pl.semaphore_signal(barrier, inc=1, device_id=partner, device_id_type=MESH)
    load_v = pltpu.make_async_copy(v_hbm, v_in, in_sem.at[0])
    load_a = pltpu.make_async_copy(a_hbm, a_in, in_sem.at[1])
    load_v.start()
    load_a.start()

    def picks(labels, count, symmetry, slots):
        chosen, taken = [], jnp.int32(0)
        for j in range(count):
            match = jnp.where(labels[j] == symmetry, 1, 0)
            chosen.append([match * jnp.where(taken == t, 1, 0) == 1 for t in range(slots)])
            taken = taken + match
        return chosen

    def pick(blocks, chosen, t):
        value = blocks[t]
        for j in range(t + 1, len(blocks)):
            value = lax.select(chosen[j][t], blocks[j], value)
        return value

    own_picks = [picks(vir_s, vir_blocks, k_s[2 * z + half], MAXB) for half in range(2)]
    row_picks = picks(occ_s, occ_blocks, k_s[lax.div(v, 4)], MAXO)

    load_a.wait()
    for t in range(MAXO):
        blocks = [a_in[:, i * BLK:(i + 1) * BLK] for i in range(occ_blocks)]
        ag[c, y, x, :, t * BLK:(t + 1) * BLK] = pick(blocks, row_picks, t)
    load_v.wait()
    for half in range(2):
        for strip in range(0, BLK, 32):
            span = slice(half * BLK + strip, half * BLK + strip + 32)
            blocks = [v_in[span, j * BLK:(j + 1) * BLK] for j in range(vir_blocks)]
            for t in range(MAXB):
                vbuf[0, span, t * BLK:(t + 1) * BLK] = pick(blocks, own_picks[half], t)

    pl.semaphore_wait(barrier, len(partners))

    rows = 2 * BLK // PIECES
    piece_order = ((0, 1, 2, 3), (2, 3, 0, 1))
    slots = ((0, 1, 2, 3, 7), (0, 4, 5, 6, 7))

    def v_copy(way, index):
        step, piece = index // PIECES, piece_order[way][index % PIECES]
        span = slice(piece * rows, (piece + 1) * rows)
        return pltpu.make_async_remote_copy(
            src_ref=vbuf.at[slots[way][step], span, :], dst_ref=vbuf.at[slots[way][step + 1], span, :],
            send_sem=vsend.at[way, index], recv_sem=vrecv.at[way, index],
            device_id=(z_next, z_prev)[way], device_id_type=MESH)

    v_count = 3 * PIECES + PIECES // 2
    v_copies = [[v_copy(way, index) for index in range(v_count)] for way in range(2)]

    def x_copy(step):
        return pltpu.make_async_remote_copy(
            src_ref=ag.at[c, y, x], dst_ref=ag.at[c, y, x], send_sem=xsend.at[step - 1], recv_sem=xrecv.at[step - 1],
            device_id=x_far[step], device_id_type=MESH)

    def y_copy(way, step):
        group = ring(y, -step if way == 0 else step, NY)
        return pltpu.make_async_remote_copy(
            src_ref=ag.at[c, group], dst_ref=ag.at[c, group], send_sem=ysend.at[way, step], recv_sem=yrecv.at[way, step],
            device_id=(y_next, y_prev)[way], device_id_type=MESH)

    def c_copy(step):
        group = ring(y, -step, NY)
        return pltpu.make_async_remote_copy(
            src_ref=ag.at[c, group], dst_ref=ag.at[c, group], send_sem=csend.at[step], recv_sem=crecv.at[step],
            device_id=twin, device_id_type=MESH)

    x_copies = [x_copy(step) for step in (1, 3, 2)]
    y_copies = [[y_copy(0, step) for step in range(4)], [y_copy(1, step) for step in range(3)]]
    c_copies = [c_copy(step) for step in range(NY)]

    for piece in range(PIECES):
        for way in range(2):
            v_copies[way][piece].start()
        if piece == 0:
            for copy in x_copies:
                copy.start()

    def v_pass(index):
        for way in range(2):
            v_copies[way][index].wait_recv()
            if index + PIECES < v_count:
                v_copies[way][index + PIECES].start()

    def y_pass(step):
        for way in range(2):
            if step <= len(y_copies[way]):
                y_copies[way][step - 1].wait_recv()
                if step < len(y_copies[way]):
                    y_copies[way][step].start()
                c_copies[step if way == 0 else NY - step].start()

    def build(group):
        for half in range(2):
            kb = group * 2 + half
            stacked = jnp.concatenate([ag[cc, group, 2 * half + xx] for xx in range(2) for cc in range(2)], axis=0)
            turned = [stacked[:, t * BLK:(t + 1) * BLK].T.astype(jnp.float32) for t in range(MAXO)]
            symmetry = k_s[kb]
            for i in range(occ_blocks):
                first = jnp.int32(0)
                for other in range(i):
                    first = first + jnp.where(occ_s[other] == occ_s[i], 1, 0)
                match = jnp.where(occ_s[i] == symmetry, 1, 0)
                scale = [(match * jnp.where(first == t, 1, 0)).astype(jnp.float32) for t in range(MAXO)]
                chosen = turned[0] * scale[0] + turned[1] * scale[1]
                amask[i * BLK:(i + 1) * BLK, pl.ds(pl.multiple_of(kb * BLK, BLK), BLK)] = chosen.astype(jnp.bfloat16)

    def product(slot, distance):
        origin = ring(z, -distance, NZ)
        left = amask[:, pl.ds(pl.multiple_of(origin * (2 * BLK), 2 * BLK), 2 * BLK)]
        return jnp.dot(left, vbuf[slot], preferred_element_type=jnp.float32)

    for copy in x_copies:
        copy.wait_recv()
    y_copies[0][0].start()
    y_copies[1][0].start()
    c_copies[0].start()
    v_pass(0)
    v_pass(1)
    y_pass(1)
    v_pass(2)
    v_pass(3)
    y_pass(2)
    v_pass(4)
    y_pass(3)
    v_pass(5)
    v_pass(6)
    y_pass(4)
    for copy in c_copies:
        copy.wait_recv()
    v_pass(7)

    @pl.loop(0, NY)
    def _(group):
        build(group)

    v_pass(8)
    acc[...] = product(0, 0)
    acc[...] += product(1, 1)
    v_pass(9)
    acc[...] += product(4, -1)
    acc[...] += product(2, 2)
    v_pass(10)
    acc[...] += product(5, -2)
    v_pass(11)
    acc[...] += product(3, 3)
    acc[...] += product(6, -3)
    v_pass(12)
    v_pass(13)
    out_ref[...] = (acc[...] + product(7, 4)).astype(out_ref.dtype)

    for copy in v_copies[0] + v_copies[1] + x_copies + y_copies[0] + y_copies[1] + c_copies:
        copy.wait_send()


def expand_kernel(occ_s, vir_s, packed, out_ref):
    symmetry = occ_s[pl.program_id(0)]
    taken = jnp.int32(0)
    for j in range(vir_s.shape[0]):
        match = vir_s[j] == symmetry
        slot = pl.multiple_of(jnp.minimum(taken, MAXB - 1) * BLK, BLK)
        block = packed[:, pl.ds(slot, BLK)]
        out_ref[:, j * BLK:(j + 1) * BLK] = lax.select(match, block, jnp.zeros_like(block))
        taken = taken + jnp.where(match, 1, 0)


def per_device(amplitudes, integrals, occ_sym, vir_sym, k_sym):
    occ_rows, part = amplitudes.shape
    depth, columns = integrals.shape
    width = MAXB * BLK
    bf16 = jnp.bfloat16
    smem = pl.BlockSpec(memory_space=pltpu.SMEM)
    anywhere = pl.BlockSpec(memory_space=pl.ANY)
    v_count = 3 * PIECES + PIECES // 2
    dma = pltpu.SemaphoreType.DMA
    packed = pl.pallas_call(
        ladder_kernel,
        out_shape=jax.ShapeDtypeStruct((occ_rows, width), bf16),
        in_specs=[smem, smem, smem, anywhere, anywhere],
        out_specs=pl.BlockSpec(memory_space=pltpu.VMEM),
        scratch_shapes=[
            pltpu.VMEM((part, occ_rows), bf16),
            pltpu.VMEM((depth, columns), bf16),
            pltpu.VMEM((2, NY, NX, part, MAXO * BLK), bf16),
            pltpu.VMEM((NZ, depth, width), bf16),
            pltpu.VMEM((occ_rows, NZ * depth), bf16),
            pltpu.VMEM((occ_rows, width), jnp.float32),
            dma((2,)),
            dma((2, v_count)), dma((2, v_count)),
            dma((3,)), dma((3,)),
            dma((2, 4)), dma((2, 4)),
            dma((NY,)), dma((NY,)),
        ],
        compiler_params=pltpu.CompilerParams(collective_id=0, has_side_effects=True),
        name="ladder_ring",
    )(occ_sym, vir_sym, k_sym, amplitudes.T, integrals)
    return pl.pallas_call(
        expand_kernel,
        grid=(occ_rows // BLK,),
        out_shape=jax.ShapeDtypeStruct((occ_rows, columns), bf16),
        in_specs=[smem, smem, pl.BlockSpec((BLK, width), lambda i: (i, 0))],
        out_specs=pl.BlockSpec((BLK, columns), lambda i: (i, 0)),
        name="expand",
    )(occ_sym, vir_sym, packed)


def solution(mesh):
    return jax.shard_map(
        per_device,
        mesh=mesh,
        in_specs=(P("occ", "vir"), P("occ", "vir"), P("occ"), P("vir"), P()),
        out_specs=P("occ", "vir"),
        check_vma=False,
    )
```

```python
import jax
import jax.numpy as jnp
from jax import lax
from jax.experimental import pallas as pl
from jax.experimental.pallas import tpu as pltpu
from jax.sharding import PartitionSpec as P

BLK = 128
MAXO = 2
MAXB = 5
NZ, NY, NX = 8, 8, 4
PIECES = 4
MESH = pl.DeviceIdType.MESH


def ladder_kernel(occ_hbm, vir_hbm, k_hbm, a_hbm, v_hbm, out_ref, occ_s, vir_s, k_s, a_in, v_in, ag, vbuf, amask, acc,
                  in_sem, vsend, vrecv, xsend, xrecv, ysend, yrecv, csend, crecv):
    occ_rows = out_ref.shape[0]
    occ_blocks = occ_rows // BLK
    vir_blocks = vir_s.shape[0]
    z = lax.axis_index("occ")
    v = lax.axis_index("vir")
    y = lax.div(v, 2 * NX)
    x = lax.rem(lax.div(v, 2), NX)
    c = lax.rem(v, 2)

    def vir_at(yy, xx, cc):
        return (yy * NX + xx) * 2 + cc

    def ring(value, step, size):
        return lax.rem(value + step + size, size)

    z_next, z_prev = (ring(z, 1, NZ), v), (ring(z, -1, NZ), v)
    y_next, y_prev = (z, vir_at(ring(y, 1, NY), x, c)), (z, vir_at(ring(y, -1, NY), x, c))
    x_far = {step: (z, vir_at(y, ring(x, step, NX), c)) for step in (1, 3, 2)}
    twin = (z, vir_at(y, x, 1 - c))
    partners = [z_next, z_prev, y_next, y_prev, twin] + list(x_far.values())

    rows = 2 * BLK // PIECES
    barrier = pltpu.get_barrier_semaphore()
    for partner in partners:
        pl.semaphore_signal(barrier, inc=1, device_id=partner, device_id_type=MESH)
    loads = [pltpu.make_async_copy(source, target, in_sem.at[index])
             for index, (source, target) in enumerate([(k_hbm, k_s), (vir_hbm, vir_s), (occ_hbm, occ_s), (a_hbm, a_in)])]
    v_loads = [pltpu.make_async_copy(v_hbm.at[piece * rows:(piece + 1) * rows], v_in.at[piece * rows:(piece + 1) * rows], in_sem.at[4 + piece])
               for piece in range(PIECES)]
    for load in loads[:3]:
        load.start()
    for piece in (0, 2, 1, 3):
        v_loads[piece].start()
    loads[3].start()
    for load in loads[:3]:
        load.wait()

    def picks(labels, count, symmetry, slots):
        chosen, taken = [], jnp.int32(0)
        for j in range(count):
            match = jnp.where(labels[j] == symmetry, 1, 0)
            chosen.append([match * jnp.where(taken == t, 1, 0) == 1 for t in range(slots)])
            taken = taken + match
        return chosen

    def pick(blocks, chosen, t):
        value = blocks[t]
        for j in range(t + 1, len(blocks)):
            value = lax.select(chosen[j][t], blocks[j], value)
        return value

    own_picks = [picks(vir_s, vir_blocks, k_s[2 * z + half], MAXB) for half in range(2)]
    row_picks = picks(occ_s, occ_blocks, k_s[lax.div(v, 4)], MAXO)

    def pack(piece):
        v_loads[piece].wait()
        for strip in range(piece * rows, (piece + 1) * rows, 32):
            span = slice(strip, strip + 32)
            blocks = [v_in[span, j * BLK:(j + 1) * BLK] for j in range(vir_blocks)]
            for t in range(MAXB):
                vbuf[0, span, t * BLK:(t + 1) * BLK] = pick(blocks, own_picks[strip // BLK], t)

    for piece in (0, 2, 1, 3):
        pack(piece)
    loads[3].wait()
    for t in range(MAXO):
        blocks = [a_in[:, i * BLK:(i + 1) * BLK] for i in range(occ_blocks)]
        ag[c, y, x, :, t * BLK:(t + 1) * BLK] = pick(blocks, row_picks, t)

    pl.semaphore_wait(barrier, len(partners))

    piece_order = ((0, 1, 2, 3), (2, 3, 0, 1))
    slots = ((0, 1, 2, 3, 7), (0, 4, 5, 6, 7))

    def v_copy(way, index):
        step, piece = index // PIECES, piece_order[way][index % PIECES]
        span = slice(piece * rows, (piece + 1) * rows)
        return pltpu.make_async_remote_copy(
            src_ref=vbuf.at[slots[way][step], span, :], dst_ref=vbuf.at[slots[way][step + 1], span, :],
            send_sem=vsend.at[way, index], recv_sem=vrecv.at[way, index],
            device_id=(z_next, z_prev)[way], device_id_type=MESH)

    v_count = 3 * PIECES + PIECES // 2
    v_copies = [[v_copy(way, index) for index in range(v_count)] for way in range(2)]

    def x_copy(step):
        return pltpu.make_async_remote_copy(
            src_ref=ag.at[c, y, x], dst_ref=ag.at[c, y, x], send_sem=xsend.at[step - 1], recv_sem=xrecv.at[step - 1],
            device_id=x_far[step], device_id_type=MESH)

    def y_copy(way, step):
        group = ring(y, -step if way == 0 else step, NY)
        return pltpu.make_async_remote_copy(
            src_ref=ag.at[c, group], dst_ref=ag.at[c, group], send_sem=ysend.at[way, step], recv_sem=yrecv.at[way, step],
            device_id=(y_next, y_prev)[way], device_id_type=MESH)

    def c_copy(step):
        group = ring(y, -step, NY)
        return pltpu.make_async_remote_copy(
            src_ref=ag.at[c, group], dst_ref=ag.at[c, group], send_sem=csend.at[step], recv_sem=crecv.at[step],
            device_id=twin, device_id_type=MESH)

    x_copies = [x_copy(step) for step in (1, 3, 2)]
    y_copies = [[y_copy(0, step) for step in range(4)], [y_copy(1, step) for step in range(3)]]
    c_copies = [c_copy(step) for step in range(NY)]

    for piece in range(PIECES):
        for way in range(2):
            v_copies[way][piece].start()
        if piece == 0:
            for copy in x_copies:
                copy.start()

    def v_pass(index):
        for way in range(2):
            v_copies[way][index].wait_recv()
            if index + PIECES < v_count:
                v_copies[way][index + PIECES].start()

    def y_pass(step):
        for way in range(2):
            if step <= len(y_copies[way]):
                y_copies[way][step - 1].wait_recv()
                if step < len(y_copies[way]):
                    y_copies[way][step].start()
                c_copies[step if way == 0 else NY - step].start()

    def build(group):
        for half in range(2):
            kb = group * 2 + half
            stacked = jnp.concatenate([ag[cc, group, 2 * half + xx] for xx in range(2) for cc in range(2)], axis=0)
            turned = [stacked[:, t * BLK:(t + 1) * BLK].T.astype(jnp.float32) for t in range(MAXO)]
            symmetry = k_s[kb]
            for i in range(occ_blocks):
                first = jnp.int32(0)
                for other in range(i):
                    first = first + jnp.where(occ_s[other] == occ_s[i], 1, 0)
                match = jnp.where(occ_s[i] == symmetry, 1, 0)
                scale = [(match * jnp.where(first == t, 1, 0)).astype(jnp.float32) for t in range(MAXO)]
                chosen = turned[0] * scale[0] + turned[1] * scale[1]
                amask[i * BLK:(i + 1) * BLK, pl.ds(pl.multiple_of(kb * BLK, BLK), BLK)] = chosen.astype(jnp.bfloat16)

    def product(slot, distance):
        origin = ring(z, -distance, NZ)
        left = amask[:, pl.ds(pl.multiple_of(origin * (2 * BLK), 2 * BLK), 2 * BLK)]
        return jnp.dot(left, vbuf[slot], preferred_element_type=jnp.float32)

    for copy in x_copies:
        copy.wait_recv()
    y_copies[0][0].start()
    y_copies[1][0].start()
    c_copies[0].start()
    v_pass(0)
    v_pass(1)
    y_pass(1)
    v_pass(2)
    v_pass(3)
    y_pass(2)
    v_pass(4)
    y_pass(3)
    v_pass(5)
    v_pass(6)
    y_pass(4)
    for copy in c_copies:
        copy.wait_recv()
    v_pass(7)

    @pl.loop(0, NY)
    def _(group):
        build(group)

    v_pass(8)
    acc[...] = product(0, 0)
    acc[...] += product(1, 1)
    v_pass(9)
    acc[...] += product(4, -1)
    acc[...] += product(2, 2)
    v_pass(10)
    acc[...] += product(5, -2)
    v_pass(11)
    acc[...] += product(3, 3)
    acc[...] += product(6, -3)
    v_pass(12)
    v_pass(13)
    out_ref[...] = (acc[...] + product(7, 4)).astype(out_ref.dtype)

    for copy in v_copies[0] + v_copies[1] + x_copies + y_copies[0] + y_copies[1] + c_copies:
        copy.wait_send()


def expand_kernel(occ_s, vir_s, packed, out_hbm, full, sems):
    copies = []
    for i in range(occ_s.shape[0]):
        span = slice(i * BLK, (i + 1) * BLK)
        taken = jnp.int32(0)
        for j in range(vir_s.shape[0]):
            match = vir_s[j] == occ_s[i]
            slot = pl.multiple_of(jnp.minimum(taken, MAXB - 1) * BLK, BLK)
            block = packed[span, pl.ds(slot, BLK)]
            full[span, j * BLK:(j + 1) * BLK] = lax.select(match, block, jnp.zeros_like(block))
            taken = taken + jnp.where(match, 1, 0)
        copies.append(pltpu.make_async_copy(full.at[span], out_hbm.at[span], sems.at[i]))
        copies[-1].start()
    for copy in copies:
        copy.wait()


def in_hbm(array):
    return pltpu.with_memory_space_constraint(array, pltpu.HBM)


def per_device(amplitudes, integrals, occ_sym, vir_sym, k_sym):
    occ_rows, part = amplitudes.shape
    depth, columns = integrals.shape
    width = MAXB * BLK
    bf16 = jnp.bfloat16
    smem = pl.BlockSpec(memory_space=pltpu.SMEM)
    vmem = pl.BlockSpec(memory_space=pltpu.VMEM)
    hbm = pl.BlockSpec(memory_space=pltpu.HBM)
    v_count = 3 * PIECES + PIECES // 2
    dma = pltpu.SemaphoreType.DMA
    occ_sym, vir_sym, k_sym = in_hbm(occ_sym), in_hbm(vir_sym), in_hbm(k_sym)
    packed = pl.pallas_call(
        ladder_kernel,
        out_shape=pltpu.VMEM((occ_rows, width), bf16),
        in_specs=[hbm] * 5,
        out_specs=vmem,
        scratch_shapes=[
            pltpu.SMEM(occ_sym.shape, jnp.int32),
            pltpu.SMEM(vir_sym.shape, jnp.int32),
            pltpu.SMEM(k_sym.shape, jnp.int32),
            pltpu.VMEM((part, occ_rows), bf16),
            pltpu.VMEM((depth, columns), bf16),
            pltpu.VMEM((2, NY, NX, part, MAXO * BLK), bf16),
            pltpu.VMEM((NZ, depth, width), bf16),
            pltpu.VMEM((occ_rows, NZ * depth), bf16),
            pltpu.VMEM((occ_rows, width), jnp.float32),
            dma((4 + PIECES,)),
            dma((2, v_count)), dma((2, v_count)),
            dma((3,)), dma((3,)),
            dma((2, 4)), dma((2, 4)),
            dma((NY,)), dma((NY,)),
        ],
        compiler_params=pltpu.CompilerParams(collective_id=0, has_side_effects=True, vmem_limit_bytes=24 << 20),
        name="ladder_ring",
    )(occ_sym, vir_sym, k_sym, in_hbm(amplitudes.T), in_hbm(integrals))
    return pl.pallas_call(
        expand_kernel,
        out_shape=jax.ShapeDtypeStruct((occ_rows, columns), bf16),
        in_specs=[smem, smem, vmem],
        out_specs=hbm,
        scratch_shapes=[pltpu.VMEM((occ_rows, columns), bf16), dma((occ_rows // BLK,))],
        compiler_params=pltpu.CompilerParams(vmem_limit_bytes=24 << 20),
        name="expand",
    )(occ_sym, vir_sym, packed)


def solution(mesh):
    return jax.shard_map(
        per_device,
        mesh=mesh,
        in_specs=(P("occ", "vir"), P("occ", "vir"), P("occ"), P("vir"), P()),
        out_specs=P("occ", "vir"),
        check_vma=False,
    )
```

```python
import jax
import jax.numpy as jnp
from jax import lax
from jax.experimental import pallas as pl
from jax.experimental.pallas import tpu as pltpu
from jax.sharding import PartitionSpec as P

BLK = 128
MAXO = 2
MAXB = 5
NZ, NY, NX = 8, 8, 4
PIECES = 4
MESH = pl.DeviceIdType.MESH


def ladder_kernel(occ_hbm, vir_hbm, k_hbm, a_hbm, v_hbm, acc, a_last, v_last, occ_s, vir_s, k_s, a_in, v_in, ag, vbuf, amask, unit,
                  in_sem, vsend, vrecv, xsend, xrecv, ysend, yrecv, csend, crecv):
    occ_rows = acc.shape[0]
    occ_blocks = occ_rows // BLK
    depth = v_hbm.shape[0]
    vir_blocks = vir_s.shape[0]
    z = lax.axis_index("occ")
    v = lax.axis_index("vir")
    y = lax.div(v, 2 * NX)
    x = lax.rem(lax.div(v, 2), NX)
    c = lax.rem(v, 2)

    def vir_at(yy, xx, cc):
        return (yy * NX + xx) * 2 + cc

    def ring(value, step, size):
        return lax.rem(value + step + size, size)

    z_next, z_prev = (ring(z, 1, NZ), v), (ring(z, -1, NZ), v)
    y_next, y_prev = (z, vir_at(ring(y, 1, NY), x, c)), (z, vir_at(ring(y, -1, NY), x, c))
    x_far = {step: (z, vir_at(y, ring(x, step, NX), c)) for step in (1, 3, 2)}
    twin = (z, vir_at(y, x, 1 - c))
    partners = [z_next, z_prev, y_next, y_prev, twin] + list(x_far.values())

    rows = 2 * BLK // PIECES
    barrier = pltpu.get_barrier_semaphore()
    for partner in partners:
        pl.semaphore_signal(barrier, inc=1, device_id=partner, device_id_type=MESH)
    loads = [pltpu.make_async_copy(source, target, in_sem.at[index])
             for index, (source, target) in enumerate([(k_hbm, k_s), (vir_hbm, vir_s), (occ_hbm, occ_s), (a_hbm, a_in)])]
    v_loads = [pltpu.make_async_copy(v_hbm.at[piece * rows:(piece + 1) * rows], v_in.at[piece * rows:(piece + 1) * rows], in_sem.at[4 + piece])
               for piece in range(PIECES)]
    for load in loads:
        load.start()
    for piece in (0, 2, 1, 3):
        v_loads[piece].start()
    for load in loads[:3]:
        load.wait()

    def picks(labels, count, symmetry, slots):
        chosen, place = [], jnp.int32(1)
        for j in range(count):
            match = labels[j] == symmetry
            code = jnp.where(match, place, 0)
            chosen.append([code == 1 << t for t in range(slots)])
            place = jnp.where(match, 2 * place, place)
        return chosen

    def pick(blocks, chosen, t):
        value = blocks[t]
        for j in range(t + 1, len(blocks)):
            value = lax.select(chosen[j][t], blocks[j], value)
        return value

    own_picks = [picks(vir_s, vir_blocks, k_s[2 * z + half], MAXB) for half in range(2)]
    row_picks = picks(occ_s, occ_blocks, k_s[lax.div(v, 4)], MAXO)

    def pack(piece):
        v_loads[piece].wait()
        for strip in range(piece * rows, (piece + 1) * rows, 32):
            span = slice(strip, strip + 32)
            blocks = [v_in[span, j * BLK:(j + 1) * BLK] for j in range(vir_blocks)]
            for t in range(MAXB):
                vbuf[span, t * BLK:(t + 1) * BLK] = pick(blocks, own_picks[strip // BLK], t)

    pack(0)
    pack(2)
    pl.semaphore_wait(barrier, len(partners))

    piece_order = ((0, 1, 2, 3), (2, 3, 0, 1))
    slots = ((0, 1, 3, 5, 7), (0, 2, 4, 6, 7))

    def v_copy(way, index):
        step, piece = index // PIECES, piece_order[way][index % PIECES]
        source, target = [slots[way][step + ahead] * depth + piece * rows for ahead in range(2)]
        return pltpu.make_async_remote_copy(
            src_ref=vbuf.at[source:source + rows], dst_ref=vbuf.at[target:target + rows],
            send_sem=vsend.at[way, index], recv_sem=vrecv.at[way, index],
            device_id=(z_next, z_prev)[way], device_id_type=MESH)

    v_counts = (3 * PIECES + PIECES // 2, 4 * PIECES)
    v_copies = [[v_copy(way, index) for index in range(v_counts[way])] for way in range(2)]

    def x_copy(step):
        return pltpu.make_async_remote_copy(
            src_ref=ag.at[c, y, x], dst_ref=ag.at[c, y, x], send_sem=xsend.at[step - 1], recv_sem=xrecv.at[step - 1],
            device_id=x_far[step], device_id_type=MESH)

    def y_copy(way, step):
        group = ring(y, -step if way == 0 else step, NY)
        return pltpu.make_async_remote_copy(
            src_ref=ag.at[c, group], dst_ref=ag.at[c, group], send_sem=ysend.at[way, step], recv_sem=yrecv.at[way, step],
            device_id=(y_next, y_prev)[way], device_id_type=MESH)

    def c_copy(step):
        group = ring(y, -step, NY)
        return pltpu.make_async_remote_copy(
            src_ref=ag.at[c, group], dst_ref=ag.at[c, group], send_sem=csend.at[step], recv_sem=crecv.at[step],
            device_id=twin, device_id_type=MESH)

    x_copies = [x_copy(step) for step in (1, 3, 2)]
    y_copies = [[y_copy(0, step) for step in range(4)], [y_copy(1, step) for step in range(3)]]
    c_copies = [c_copy(step) for step in range(NY)]

    v_copies[0][0].start()
    v_copies[1][0].start()
    loads[3].wait()
    for t in range(MAXO):
        blocks = [a_in[:, i * BLK:(i + 1) * BLK] for i in range(occ_blocks)]
        ag[c, y, x, :, t * BLK:(t + 1) * BLK] = pick(blocks, row_picks, t)
    pack(1)
    pack(3)
    for copy in x_copies:
        copy.start()
    for index in range(1, PIECES):
        for way in range(2):
            v_copies[way][index].start()

    def when(holds, action):
        if holds is True:
            action()
        elif holds is not False:
            pl.when(holds)(action)

    def far(way, index, receiver):
        if index < 3 * PIECES:
            return True
        if way == 0:
            return receiver != 0
        return True if index < 3 * PIECES + PIECES // 2 else receiver == 0

    receivers = (ring(z, 1, NZ), ring(z, -1, NZ))

    def v_pass(index):
        for way in range(2):
            if index < len(v_copies[way]):
                when(far(way, index, z), v_copies[way][index].wait_recv)
            if index + PIECES < len(v_copies[way]):
                when(far(way, index + PIECES, receivers[way]), v_copies[way][index + PIECES].start)

    def y_pass(step):
        for way in range(2):
            if step <= len(y_copies[way]):
                y_copies[way][step - 1].wait_recv()
                if step < len(y_copies[way]):
                    y_copies[way][step].start()
                c_copies[step if way == 0 else NY - step].start()

    ranks = []
    for i in range(occ_blocks):
        rank = jnp.int32(0)
        for other in range(i):
            rank = rank + jnp.where(occ_s[other] == occ_s[i], 1, 0)
        ranks.append(rank)

    def build(step):
        c_copies[step].wait_recv()
        group = ring(y, -step, NY)
        distance = ring(z, -group, NZ)
        slot = 2 * jnp.minimum(distance, NZ - distance) - jnp.where((distance > 0) & (distance <= NZ // 2), 1, 0)
        nothing = jnp.zeros((BLK, BLK), jnp.bfloat16)
        for half in range(2):
            kb = group * 2 + half
            stacked = jnp.concatenate([ag[cc, group, 2 * half + xx] for xx in range(2) for cc in range(2)], axis=0)
            turned = lax.dot_general(unit[...], stacked, (((1,), (1,)), ((), ())), preferred_element_type=jnp.float32).astype(jnp.bfloat16)
            symmetry = k_s[kb]
            for i in range(occ_blocks):
                chosen = lax.select(ranks[i] == 0, turned[:BLK], turned[BLK:])
                amask[i * BLK:(i + 1) * BLK, pl.ds(pl.multiple_of(slot * depth + half * BLK, BLK), BLK)] = lax.select(occ_s[i] == symmetry, chosen, nothing)

    def product(first, last):
        return jnp.dot(amask[:, first * depth:last * depth], vbuf[first * depth:last * depth], preferred_element_type=jnp.float32)

    diagonal = [lax.broadcasted_iota(jnp.int32, unit.shape, axis) for axis in range(2)]
    unit[...] = (diagonal[0] == diagonal[1]).astype(jnp.bfloat16)
    v_pass(0)
    for copy in x_copies:
        copy.wait_recv()
    y_copies[0][0].start()
    y_copies[1][0].start()
    c_copies[0].start()
    v_pass(1)
    v_pass(2)
    y_pass(1)
    v_pass(3)
    v_pass(4)
    y_pass(2)
    build(0)
    v_pass(5)
    y_pass(3)
    build(1)
    build(7)
    v_pass(6)
    v_pass(7)
    y_pass(4)
    build(2)
    build(6)
    v_pass(8)
    build(3)
    build(5)
    v_pass(9)
    v_pass(10)
    v_pass(11)
    build(4)
    a_last[...] = amask[:, 7 * depth:]
    acc[...] = product(0, 5)
    acc[...] += product(5, 7)
    for index in range(3 * PIECES, 4 * PIECES):
        v_pass(index)
    v_last[...] = vbuf[7 * depth:]

    for way in range(2):
        for index, copy in enumerate(v_copies[way]):
            when(far(way, index, receivers[way]), copy.wait_send)
    for copy in x_copies + y_copies[0] + y_copies[1] + c_copies:
        copy.wait_send()


def expand_kernel(occ_hbm, vir_hbm, acc, a_last, v_last, out_hbm, occ_s, vir_s, packed, full, sems):
    labels = [pltpu.make_async_copy(occ_hbm, occ_s, sems.at[0]), pltpu.make_async_copy(vir_hbm, vir_s, sems.at[1])]
    for copy in labels:
        copy.start()
    copies = []
    for i in range(occ_s.shape[0]):
        span = slice(i * BLK, (i + 1) * BLK)
        rest = jnp.dot(a_last[span, :], v_last[...], preferred_element_type=jnp.float32)
        packed[i] = (acc[span, :] + rest).astype(packed.dtype)
        if i == 0:
            for copy in labels:
                copy.wait()
        taken = jnp.int32(0)
        for j in range(vir_s.shape[0]):
            match = vir_s[j] == occ_s[i]
            slot = pl.multiple_of(jnp.minimum(taken, MAXB - 1) * BLK, BLK)
            block = packed[i, :, pl.ds(slot, BLK)]
            full[span, j * BLK:(j + 1) * BLK] = lax.select(match, block, jnp.zeros_like(block))
            taken = taken + jnp.where(match, 1, 0)
        copies.append(pltpu.make_async_copy(full.at[span], out_hbm.at[span], sems.at[2 + i]))
        copies[-1].start()
    for copy in copies:
        copy.wait()


def in_hbm(array):
    return pltpu.with_memory_space_constraint(array, pltpu.HBM)


def per_device(amplitudes, integrals, occ_sym, vir_sym, k_sym):
    occ_rows, part = amplitudes.shape
    depth, columns = integrals.shape
    width = MAXB * BLK
    bf16 = jnp.bfloat16
    vmem = pl.BlockSpec(memory_space=pltpu.VMEM)
    hbm = pl.BlockSpec(memory_space=pltpu.HBM)
    v_count = 4 * PIECES
    dma = pltpu.SemaphoreType.DMA
    occ_sym, vir_sym, k_sym = in_hbm(occ_sym), in_hbm(vir_sym), in_hbm(k_sym)
    parts = pl.pallas_call(
        ladder_kernel,
        out_shape=(pltpu.VMEM((occ_rows, width), jnp.float32), pltpu.VMEM((occ_rows, depth), bf16), pltpu.VMEM((depth, width), bf16)),
        in_specs=[hbm] * 5,
        out_specs=(vmem,) * 3,
        scratch_shapes=[
            pltpu.SMEM(occ_sym.shape, jnp.int32),
            pltpu.SMEM(vir_sym.shape, jnp.int32),
            pltpu.SMEM(k_sym.shape, jnp.int32),
            pltpu.VMEM((part, occ_rows), bf16),
            pltpu.VMEM((depth, columns), bf16),
            pltpu.VMEM((2, NY, NX, part, MAXO * BLK), bf16),
            pltpu.VMEM((NZ * depth, width), bf16),
            pltpu.VMEM((occ_rows, NZ * depth), bf16),
            pltpu.VMEM((MAXO * BLK, MAXO * BLK), bf16),
            dma((4 + PIECES,)),
            dma((2, v_count)), dma((2, v_count)),
            dma((3,)), dma((3,)),
            dma((2, 4)), dma((2, 4)),
            dma((NY,)), dma((NY,)),
        ],
        compiler_params=pltpu.CompilerParams(collective_id=0, has_side_effects=True, vmem_limit_bytes=24 << 20),
        name="ladder_ring",
    )(occ_sym, vir_sym, k_sym, in_hbm(amplitudes.T), in_hbm(integrals))
    return pl.pallas_call(
        expand_kernel,
        out_shape=jax.ShapeDtypeStruct((occ_rows, columns), bf16),
        in_specs=[hbm, hbm, vmem, vmem, vmem],
        out_specs=hbm,
        scratch_shapes=[
            pltpu.SMEM(occ_sym.shape, jnp.int32),
            pltpu.SMEM(vir_sym.shape, jnp.int32),
            pltpu.VMEM((occ_rows // BLK, BLK, width), bf16),
            pltpu.VMEM((occ_rows, columns), bf16),
            dma((2 + occ_rows // BLK,)),
        ],
        compiler_params=pltpu.CompilerParams(vmem_limit_bytes=24 << 20),
        name="expand",
    )(occ_sym, vir_sym, *parts)


def solution(mesh):
    return jax.shard_map(
        per_device,
        mesh=mesh,
        in_specs=(P("occ", "vir"), P("occ", "vir"), P("occ"), P("vir"), P()),
        out_specs=P("occ", "vir"),
        check_vma=False,
    )
```

```python
import jax
import jax.numpy as jnp
from jax import lax
from jax.experimental import pallas as pl
from jax.experimental.pallas import tpu as pltpu
from jax.sharding import PartitionSpec as P

BLK = 128
MAXO = 2
MAXB = 5
NZ, NY, NX = 8, 8, 4
PIECES = 4
FIRST_ORDER = "v1vv2v3vv4vxvvcbbvbbvbbvbb"
ORDER = "v1vv2v3vv4vvxvvvvcbbbbbbbb"
MESH = pl.DeviceIdType.MESH


def ladder_kernel(occ_hbm, vir_hbm, k_hbm, a_hbm, v_hbm, acc, a_last, v_last, occ_s, vir_s, k_s, a_in, v_in, ag, vbuf, amask, unit,
                  in_sem, vsend, vrecv, xsend, xrecv, ysend, yrecv, csend, crecv):
    occ_rows = acc.shape[0]
    occ_blocks = occ_rows // BLK
    depth = v_hbm.shape[0]
    vir_blocks = vir_s.shape[0]
    z = lax.axis_index("occ")
    v = lax.axis_index("vir")
    y = lax.div(v, 2 * NX)
    x = lax.rem(lax.div(v, 2), NX)
    c = lax.rem(v, 2)

    def vir_at(yy, xx, cc):
        return (yy * NX + xx) * 2 + cc

    def ring(value, step, size):
        return lax.rem(value + step + size, size)

    z_next, z_prev = (ring(z, 1, NZ), v), (ring(z, -1, NZ), v)
    y_next, y_prev = (z, vir_at(ring(y, 1, NY), x, c)), (z, vir_at(ring(y, -1, NY), x, c))
    x_far = {step: (z, vir_at(y, ring(x, step, NX), c)) for step in (1, 3, 2)}
    twin = (z, vir_at(y, x, 1 - c))
    partners = [z_next, z_prev, y_next, y_prev, twin] + list(x_far.values())

    rows = 2 * BLK // PIECES
    barrier = pltpu.get_barrier_semaphore()
    for partner in partners:
        pl.semaphore_signal(barrier, inc=1, device_id=partner, device_id_type=MESH)
    loads = [pltpu.make_async_copy(source, target, in_sem.at[index])
             for index, (source, target) in enumerate([(k_hbm, k_s), (vir_hbm, vir_s), (occ_hbm, occ_s), (a_hbm, a_in)])]
    v_loads = [pltpu.make_async_copy(v_hbm.at[piece * rows:(piece + 1) * rows], v_in.at[piece * rows:(piece + 1) * rows], in_sem.at[4 + piece])
               for piece in range(PIECES)]
    for load in loads:
        load.start()
    for piece in (0, 2, 1, 3):
        v_loads[piece].start()
    for load in loads[:3]:
        load.wait()

    def picks(labels, count, symmetry, slots):
        chosen, place = [], jnp.int32(1)
        for j in range(count):
            match = labels[j] == symmetry
            code = jnp.where(match, place, 0)
            chosen.append([code == 1 << t for t in range(slots)])
            place = jnp.where(match, 2 * place, place)
        return chosen

    def pick(blocks, chosen, t):
        value = blocks[t]
        for j in range(t + 1, len(blocks)):
            value = lax.select(chosen[j][t], blocks[j], value)
        return value

    own_picks = [picks(vir_s, vir_blocks, k_s[2 * z + half], MAXB) for half in range(2)]
    row_picks = picks(occ_s, occ_blocks, k_s[lax.div(v, 4)], MAXO)

    def pack(piece):
        v_loads[piece].wait()
        for strip in range(piece * rows, (piece + 1) * rows, 32):
            span = slice(strip, strip + 32)
            blocks = [v_in[span, j * BLK:(j + 1) * BLK] for j in range(vir_blocks)]
            for t in range(MAXB):
                vbuf[span, t * BLK:(t + 1) * BLK] = pick(blocks, own_picks[strip // BLK], t)

    pack(0)
    pack(2)
    pl.semaphore_wait(barrier, len(partners))

    piece_order = ((0, 1, 2, 3), (2, 3, 0, 1))
    slots = ((0, 1, 3, 5, 7), (0, 2, 4, 6, 7))

    def v_copy(way, index):
        step, piece = index // PIECES, piece_order[way][index % PIECES]
        source, target = [slots[way][step + ahead] * depth + piece * rows for ahead in range(2)]
        return pltpu.make_async_remote_copy(
            src_ref=vbuf.at[source:source + rows], dst_ref=vbuf.at[target:target + rows],
            send_sem=vsend.at[way, index], recv_sem=vrecv.at[way, index],
            device_id=(z_next, z_prev)[way], device_id_type=MESH)

    v_counts = (3 * PIECES + PIECES // 2, 4 * PIECES)
    v_copies = [[v_copy(way, index) for index in range(v_counts[way])] for way in range(2)]

    def y_copy(way, step):
        group = ring(y, -step if way == 0 else step, NY)
        return pltpu.make_async_remote_copy(
            src_ref=ag.at[c, x, group], dst_ref=ag.at[c, x, group], send_sem=ysend.at[way, step], recv_sem=yrecv.at[way, step],
            device_id=(y_next, y_prev)[way], device_id_type=MESH)

    def x_copy(step, group):
        part_of = ag.at[c, x] if group is None else ag.at[c, x, group]
        return pltpu.make_async_remote_copy(
            src_ref=part_of, dst_ref=part_of, send_sem=xsend.at[step - 1], recv_sem=xrecv.at[step - 1],
            device_id=x_far[step], device_id_type=MESH)

    def c_copy(step):
        column = ring(x, step, NX)
        return pltpu.make_async_remote_copy(
            src_ref=ag.at[c, column], dst_ref=ag.at[c, column], send_sem=csend.at[step], recv_sem=crecv.at[step],
            device_id=twin, device_id_type=MESH)

    y_copies = [[y_copy(0, step) for step in range(4)], [y_copy(1, step) for step in range(3)]]
    x_whole = [x_copy(step, None) for step in (1, 3, 2)]
    c_copies = [c_copy(step) for step in range(NX)]

    def x_send(step):
        group = ring(y, step, NY)
        for target in (1, 3, 2):
            x_copy(target, group).start()

    v_copies[0][0].start()
    v_copies[1][0].start()
    loads[3].wait()
    for t in range(MAXO):
        blocks = [a_in[:, i * BLK:(i + 1) * BLK] for i in range(occ_blocks)]
        ag[c, x, y, :, t * BLK:(t + 1) * BLK] = pick(blocks, row_picks, t)
    pack(1)
    pack(3)
    y_copies[0][0].start()
    y_copies[1][0].start()
    x_send(0)
    for index in range(1, PIECES):
        for way in range(2):
            v_copies[way][index].start()

    def when(holds, action):
        if holds is True:
            action()
        elif holds is not False:
            pl.when(holds)(action)

    def far(way, index, receiver):
        if index < 3 * PIECES:
            return True
        if way == 0:
            return receiver != 0
        return True if index < 3 * PIECES + PIECES // 2 else receiver == 0

    receivers = (ring(z, 1, NZ), ring(z, -1, NZ))

    def v_pass(index):
        for way in (1, 0):
            if index < len(v_copies[way]):
                when(far(way, index, z), v_copies[way][index].wait_recv)
            if index + PIECES < len(v_copies[way]):
                when(far(way, index + PIECES, receivers[way]), v_copies[way][index + PIECES].start)

    def y_pass(step):
        for way in range(2):
            if step <= len(y_copies[way]):
                y_copies[way][step - 1].wait_recv()
                if step < len(y_copies[way]):
                    y_copies[way][step].start()
                x_send(-step if way == 0 else step)
        if step == NY // 2:
            c_copies[0].start()

    ranks = []
    for i in range(occ_blocks):
        rank = jnp.int32(0)
        for other in range(i):
            rank = rank + jnp.where(occ_s[other] == occ_s[i], 1, 0)
        ranks.append(rank)

    def build(step):
        group = ring(y, -step, NY)
        distance = ring(z, -group, NZ)
        slot = 2 * jnp.minimum(distance, NZ - distance) - jnp.where((distance > 0) & (distance <= NZ // 2), 1, 0)
        nothing = jnp.zeros((BLK, BLK), jnp.bfloat16)
        for half in range(2):
            kb = group * 2 + half
            stacked = jnp.concatenate([ag[cc, 2 * half + xx, group] for xx in range(2) for cc in range(2)], axis=0)
            turned = lax.dot_general(unit[...], stacked, (((1,), (1,)), ((), ())), preferred_element_type=jnp.float32).astype(jnp.bfloat16)
            symmetry = k_s[kb]
            for i in range(occ_blocks):
                chosen = lax.select(ranks[i] == 0, turned[:BLK], turned[BLK:])
                amask[i * BLK:(i + 1) * BLK, pl.ds(pl.multiple_of(slot * depth + half * BLK, BLK), BLK)] = lax.select(occ_s[i] == symmetry, chosen, nothing)

    def product(first, last):
        return jnp.dot(amask[:, first * depth:last * depth], vbuf[first * depth:last * depth], preferred_element_type=jnp.float32)

    diagonal = [lax.broadcasted_iota(jnp.int32, unit.shape, axis) for axis in range(2)]
    unit[...] = (diagonal[0] == diagonal[1]).astype(jnp.bfloat16)
    def x_pass():
        for copy in x_whole:
            copy.wait_recv()
        for copy in c_copies[1:]:
            copy.start()

    def c_pass():
        for copy in c_copies:
            copy.wait_recv()

    def run(order):
        ring_steps, builds = iter(range(4 * PIECES)), iter((0, 1, 7, 2, 6, 3, 5, 4))
        for event in order:
            if event == "v":
                v_pass(next(ring_steps))
            elif event == "x":
                x_pass()
            elif event == "c":
                c_pass()
            elif event == "b":
                build(next(builds))
            else:
                y_pass(int(event))

    pl.when(z == 0)(lambda: run(FIRST_ORDER))
    pl.when(z != 0)(lambda: run(ORDER))
    a_last[...] = amask[:, 7 * depth:]
    acc[...] = product(0, 7)
    for index in range(3 * PIECES, 4 * PIECES):
        v_pass(index)
    v_last[...] = vbuf[7 * depth:]

    for way in range(2):
        for index, copy in enumerate(v_copies[way]):
            when(far(way, index, receivers[way]), copy.wait_send)
    for copy in x_whole + y_copies[0] + y_copies[1] + c_copies:
        copy.wait_send()


def expand_kernel(occ_hbm, vir_hbm, acc, a_last, v_last, out_hbm, occ_s, vir_s, packed, full, sems):
    labels = [pltpu.make_async_copy(occ_hbm, occ_s, sems.at[0]), pltpu.make_async_copy(vir_hbm, vir_s, sems.at[1])]
    for copy in labels:
        copy.start()
    copies = []
    for i in range(occ_s.shape[0]):
        span = slice(i * BLK, (i + 1) * BLK)
        rest = jnp.dot(a_last[span, :], v_last[...], preferred_element_type=jnp.float32)
        packed[i] = (acc[span, :] + rest).astype(packed.dtype)
        if i == 0:
            for copy in labels:
                copy.wait()
        taken = jnp.int32(0)
        for j in range(vir_s.shape[0]):
            match = vir_s[j] == occ_s[i]
            slot = pl.multiple_of(jnp.minimum(taken, MAXB - 1) * BLK, BLK)
            block = packed[i, :, pl.ds(slot, BLK)]
            full[span, j * BLK:(j + 1) * BLK] = lax.select(match, block, jnp.zeros_like(block))
            taken = taken + jnp.where(match, 1, 0)
        copies.append(pltpu.make_async_copy(full.at[span], out_hbm.at[span], sems.at[2 + i]))
        copies[-1].start()
    for copy in copies:
        copy.wait()


def in_hbm(array):
    return pltpu.with_memory_space_constraint(array, pltpu.HBM)


def per_device(amplitudes, integrals, occ_sym, vir_sym, k_sym):
    occ_rows, part = amplitudes.shape
    depth, columns = integrals.shape
    width = MAXB * BLK
    bf16 = jnp.bfloat16
    vmem = pl.BlockSpec(memory_space=pltpu.VMEM)
    hbm = pl.BlockSpec(memory_space=pltpu.HBM)
    v_count = 4 * PIECES
    dma = pltpu.SemaphoreType.DMA
    occ_sym, vir_sym, k_sym = in_hbm(occ_sym), in_hbm(vir_sym), in_hbm(k_sym)
    parts = pl.pallas_call(
        ladder_kernel,
        out_shape=(pltpu.VMEM((occ_rows, width), jnp.float32), pltpu.VMEM((occ_rows, depth), bf16), pltpu.VMEM((depth, width), bf16)),
        in_specs=[hbm] * 5,
        out_specs=(vmem,) * 3,
        scratch_shapes=[
            pltpu.SMEM(occ_sym.shape, jnp.int32),
            pltpu.SMEM(vir_sym.shape, jnp.int32),
            pltpu.SMEM(k_sym.shape, jnp.int32),
            pltpu.VMEM((part, occ_rows), bf16),
            pltpu.VMEM((depth, columns), bf16),
            pltpu.VMEM((2, NX, NY, part, MAXO * BLK), bf16),
            pltpu.VMEM((NZ * depth, width), bf16),
            pltpu.VMEM((occ_rows, NZ * depth), bf16),
            pltpu.VMEM((MAXO * BLK, MAXO * BLK), bf16),
            dma((4 + PIECES,)),
            dma((2, v_count)), dma((2, v_count)),
            dma((3,)), dma((3,)),
            dma((2, 4)), dma((2, 4)),
            dma((NX,)), dma((NX,)),
        ],
        compiler_params=pltpu.CompilerParams(collective_id=0, has_side_effects=True, vmem_limit_bytes=24 << 20),
        name="ladder_ring",
    )(occ_sym, vir_sym, k_sym, in_hbm(amplitudes.T), in_hbm(integrals))
    return pl.pallas_call(
        expand_kernel,
        out_shape=jax.ShapeDtypeStruct((occ_rows, columns), bf16),
        in_specs=[hbm, hbm, vmem, vmem, vmem],
        out_specs=hbm,
        scratch_shapes=[
            pltpu.SMEM(occ_sym.shape, jnp.int32),
            pltpu.SMEM(vir_sym.shape, jnp.int32),
            pltpu.VMEM((occ_rows // BLK, BLK, width), bf16),
            pltpu.VMEM((occ_rows, columns), bf16),
            dma((2 + occ_rows // BLK,)),
        ],
        compiler_params=pltpu.CompilerParams(vmem_limit_bytes=24 << 20),
        name="expand",
    )(occ_sym, vir_sym, *parts)


def solution(mesh):
    return jax.shard_map(
        per_device,
        mesh=mesh,
        in_specs=(P("occ", "vir"), P("occ", "vir"), P("occ"), P("vir"), P()),
        out_specs=P("occ", "vir"),
        check_vma=False,
    )
```

```python
import jax
import jax.numpy as jnp
from jax import lax
from jax.experimental import pallas as pl
from jax.experimental.pallas import tpu as pltpu
from jax.sharding import PartitionSpec as P

BLK = 128
MAXO = 2
MAXB = 5
NZ, NY, NX = 8, 8, 4
PIECES = 4
FIRST_ORDER = "v1vv2v3vv4vxvvcbbvbbvbbvbb"
ORDER = "v1vv2v3vv4vvxvvvvcbbbbbbbb"
MESH = pl.DeviceIdType.MESH


def ladder_kernel(occ_hbm, vir_hbm, k_hbm, a_hbm, v_hbm, acc, a_last, v_last, occ_out, vir_out, occ_s, vir_s, k_s, a_in, v_in, ag, vbuf, amask, unit,
                  in_sem, vsend, vrecv, xsend, xrecv, ysend, yrecv, csend, crecv):
    occ_rows = acc.shape[0]
    occ_blocks = occ_rows // BLK
    depth = v_hbm.shape[0]
    vir_blocks = vir_s.shape[0]
    z = lax.axis_index("occ")
    v = lax.axis_index("vir")
    y = lax.div(v, 2 * NX)
    x = lax.rem(lax.div(v, 2), NX)
    c = lax.rem(v, 2)

    def vir_at(yy, xx, cc):
        return (yy * NX + xx) * 2 + cc

    def ring(value, step, size):
        return lax.rem(value + step + size, size)

    z_next, z_prev = (ring(z, 1, NZ), v), (ring(z, -1, NZ), v)
    y_next, y_prev = (z, vir_at(ring(y, 1, NY), x, c)), (z, vir_at(ring(y, -1, NY), x, c))
    x_far = {step: (z, vir_at(y, ring(x, step, NX), c)) for step in (1, 3, 2)}
    twin = (z, vir_at(y, x, 1 - c))
    partners = [z_next, z_prev, y_next, y_prev, twin] + list(x_far.values())

    rows = 2 * BLK // PIECES
    barrier = pltpu.get_barrier_semaphore()
    for partner in partners:
        pl.semaphore_signal(barrier, inc=1, device_id=partner, device_id_type=MESH)
    loads = [pltpu.make_async_copy(source, target, in_sem.at[index])
             for index, (source, target) in enumerate([(k_hbm, k_s), (vir_hbm, vir_s), (occ_hbm, occ_s), (a_hbm, a_in)])]
    v_loads = [pltpu.make_async_copy(v_hbm.at[piece * rows:(piece + 1) * rows], v_in.at[piece * rows:(piece + 1) * rows], in_sem.at[4 + piece])
               for piece in range(PIECES)]
    for load in loads:
        load.start()
    for piece in (0, 2, 1, 3):
        v_loads[piece].start()
    for load in loads[:3]:
        load.wait()

    def picks(labels, count, symmetry, slots):
        chosen, place = [], jnp.int32(1)
        for j in range(count):
            match = labels[j] == symmetry
            code = jnp.where(match, place, 0)
            chosen.append([code == 1 << t for t in range(slots)])
            place = jnp.where(match, 2 * place, place)
        return chosen

    def pick(blocks, chosen, t):
        value = blocks[t]
        for j in range(t + 1, len(blocks)):
            value = lax.select(chosen[j][t], blocks[j], value)
        return value

    own_picks = [picks(vir_s, vir_blocks, k_s[2 * z + half], MAXB) for half in range(2)]
    row_picks = picks(occ_s, occ_blocks, k_s[lax.div(v, 4)], MAXO)

    def pack(piece):
        v_loads[piece].wait()
        for strip in range(piece * rows, (piece + 1) * rows, 32):
            span = slice(strip, strip + 32)
            blocks = [v_in[span, j * BLK:(j + 1) * BLK] for j in range(vir_blocks)]
            for t in range(MAXB):
                vbuf[span, t * BLK:(t + 1) * BLK] = pick(blocks, own_picks[strip // BLK], t)

    pack(0)
    pack(2)
    pl.semaphore_wait(barrier, len(partners))

    piece_order = ((0, 1, 2, 3), (2, 3, 0, 1))
    slots = ((0, 1, 3, 5, 7), (0, 2, 4, 6, 7))

    def v_copy(way, index):
        step, piece = index // PIECES, piece_order[way][index % PIECES]
        source, target = [slots[way][step + ahead] * depth + piece * rows for ahead in range(2)]
        return pltpu.make_async_remote_copy(
            src_ref=vbuf.at[source:source + rows], dst_ref=vbuf.at[target:target + rows],
            send_sem=vsend.at[way, index], recv_sem=vrecv.at[way, index],
            device_id=(z_next, z_prev)[way], device_id_type=MESH)

    v_counts = (3 * PIECES + PIECES // 2, 4 * PIECES)
    v_copies = [[v_copy(way, index) for index in range(v_counts[way])] for way in range(2)]

    def y_copy(way, step):
        group = ring(y, -step if way == 0 else step, NY)
        return pltpu.make_async_remote_copy(
            src_ref=ag.at[c, x, group], dst_ref=ag.at[c, x, group], send_sem=ysend.at[way, step], recv_sem=yrecv.at[way, step],
            device_id=(y_next, y_prev)[way], device_id_type=MESH)

    def x_copy(step, group):
        part_of = ag.at[c, x] if group is None else ag.at[c, x, group]
        return pltpu.make_async_remote_copy(
            src_ref=part_of, dst_ref=part_of, send_sem=xsend.at[step - 1], recv_sem=xrecv.at[step - 1],
            device_id=x_far[step], device_id_type=MESH)

    def c_copy(step):
        column = ring(x, step, NX)
        return pltpu.make_async_remote_copy(
            src_ref=ag.at[c, column], dst_ref=ag.at[c, column], send_sem=csend.at[step], recv_sem=crecv.at[step],
            device_id=twin, device_id_type=MESH)

    y_copies = [[y_copy(0, step) for step in range(4)], [y_copy(1, step) for step in range(3)]]
    x_whole = [x_copy(step, None) for step in (1, 3, 2)]
    c_copies = [c_copy(step) for step in range(NX)]

    def x_send(step):
        group = ring(y, step, NY)
        for target in (1, 3, 2):
            x_copy(target, group).start()

    v_copies[0][0].start()
    v_copies[1][0].start()
    loads[3].wait()
    for t in range(MAXO):
        blocks = [a_in[:, i * BLK:(i + 1) * BLK] for i in range(occ_blocks)]
        ag[c, x, y, :, t * BLK:(t + 1) * BLK] = pick(blocks, row_picks, t)
    pack(1)
    pack(3)
    y_copies[0][0].start()
    y_copies[1][0].start()
    x_send(0)
    for index in range(1, PIECES):
        for way in range(2):
            v_copies[way][index].start()

    def when(holds, action):
        if holds is True:
            action()
        elif holds is not False:
            pl.when(holds)(action)

    def far(way, index, receiver):
        if index < 3 * PIECES:
            return True
        if way == 0:
            return receiver != 0
        return True if index < 3 * PIECES + PIECES // 2 else receiver == 0

    receivers = (ring(z, 1, NZ), ring(z, -1, NZ))

    def v_pass(index):
        for way in (1, 0):
            if index < len(v_copies[way]):
                when(far(way, index, z), v_copies[way][index].wait_recv)
            if index + PIECES < len(v_copies[way]):
                when(far(way, index + PIECES, receivers[way]), v_copies[way][index + PIECES].start)

    def y_pass(step):
        for way in range(2):
            if step <= len(y_copies[way]):
                y_copies[way][step - 1].wait_recv()
                if step < len(y_copies[way]):
                    y_copies[way][step].start()
                x_send(-step if way == 0 else step)
        if step == NY // 2:
            c_copies[0].start()

    ranks = []
    for i in range(occ_blocks):
        rank = jnp.int32(0)
        for other in range(i):
            rank = rank + jnp.where(occ_s[other] == occ_s[i], 1, 0)
        ranks.append(rank)

    def build(step):
        group = ring(y, -step, NY)
        distance = ring(z, -group, NZ)
        slot = 2 * jnp.minimum(distance, NZ - distance) - jnp.where((distance > 0) & (distance <= NZ // 2), 1, 0)
        nothing = jnp.zeros((BLK, BLK), jnp.bfloat16)
        for half in range(2):
            kb = group * 2 + half
            stacked = jnp.concatenate([ag[cc, 2 * half + xx, group] for xx in range(2) for cc in range(2)], axis=0)
            turned = lax.dot_general(unit[...], stacked, (((1,), (1,)), ((), ())), preferred_element_type=jnp.float32).astype(jnp.bfloat16)
            symmetry = k_s[kb]
            for i in range(occ_blocks):
                chosen = lax.select(ranks[i] == 0, turned[:BLK], turned[BLK:])
                amask[i * BLK:(i + 1) * BLK, pl.ds(pl.multiple_of(slot * depth + half * BLK, BLK), BLK)] = lax.select(occ_s[i] == symmetry, chosen, nothing)

    def product(first, last):
        return jnp.dot(amask[:, first * depth:last * depth], vbuf[first * depth:last * depth], preferred_element_type=jnp.float32)

    for i in range(occ_blocks):
        occ_out[i] = occ_s[i]
    for j in range(vir_blocks):
        vir_out[j] = vir_s[j]
    diagonal = [lax.broadcasted_iota(jnp.int32, unit.shape, axis) for axis in range(2)]
    unit[...] = (diagonal[0] == diagonal[1]).astype(jnp.bfloat16)
    def x_pass():
        for copy in x_whole:
            copy.wait_recv()
        for copy in c_copies[1:]:
            copy.start()

    def c_pass():
        for copy in c_copies:
            copy.wait_recv()

    def run(order):
        ring_steps, builds = iter(range(4 * PIECES)), iter((0, 1, 7, 2, 6, 3, 5, 4))
        for event in order:
            if event == "v":
                v_pass(next(ring_steps))
            elif event == "x":
                x_pass()
            elif event == "c":
                c_pass()
            elif event == "b":
                build(next(builds))
            else:
                y_pass(int(event))

    pl.when(z == 0)(lambda: run(FIRST_ORDER))
    pl.when(z != 0)(lambda: run(ORDER))
    a_last[...] = amask[:, 7 * depth:]
    acc[...] = product(0, 7)
    for index in range(3 * PIECES, 4 * PIECES):
        v_pass(index)
    v_last[...] = vbuf[7 * depth:]

    for way in range(2):
        for index, copy in enumerate(v_copies[way]):
            when(far(way, index, receivers[way]), copy.wait_send)
    for copy in x_whole + y_copies[0] + y_copies[1] + c_copies:
        copy.wait_send()


def expand_kernel(acc, a_last, v_last, occ_s, vir_s, out_hbm, packed, full, sems):
    copies = []
    for i in range(occ_s.shape[0]):
        span = slice(i * BLK, (i + 1) * BLK)
        rest = jnp.dot(a_last[span, :], v_last[...], preferred_element_type=jnp.float32)
        packed[i] = (acc[span, :] + rest).astype(packed.dtype)
        taken = jnp.int32(0)
        for j in range(vir_s.shape[0]):
            match = vir_s[j] == occ_s[i]
            slot = pl.multiple_of(jnp.minimum(taken, MAXB - 1) * BLK, BLK)
            block = packed[i, :, pl.ds(slot, BLK)]
            full[span, j * BLK:(j + 1) * BLK] = lax.select(match, block, jnp.zeros_like(block))
            taken = taken + jnp.where(match, 1, 0)
        copies.append(pltpu.make_async_copy(full.at[span], out_hbm.at[span], sems.at[2 + i]))
        copies[-1].start()
    for copy in copies:
        copy.wait()


def in_hbm(array):
    return pltpu.with_memory_space_constraint(array, pltpu.HBM)


def per_device(amplitudes, integrals, occ_sym, vir_sym, k_sym):
    occ_rows, part = amplitudes.shape
    depth, columns = integrals.shape
    width = MAXB * BLK
    bf16 = jnp.bfloat16
    vmem = pl.BlockSpec(memory_space=pltpu.VMEM)
    hbm = pl.BlockSpec(memory_space=pltpu.HBM)
    smem = pl.BlockSpec(memory_space=pltpu.SMEM)
    v_count = 4 * PIECES
    dma = pltpu.SemaphoreType.DMA
    occ_sym, vir_sym, k_sym = in_hbm(occ_sym), in_hbm(vir_sym), in_hbm(k_sym)
    parts = pl.pallas_call(
        ladder_kernel,
        out_shape=(pltpu.VMEM((occ_rows, width), jnp.float32), pltpu.VMEM((occ_rows, depth), bf16), pltpu.VMEM((depth, width), bf16), pltpu.SMEM(occ_sym.shape, jnp.int32), pltpu.SMEM(vir_sym.shape, jnp.int32)),
        in_specs=[hbm] * 5,
        out_specs=(vmem,) * 3 + (smem,) * 2,
        scratch_shapes=[
            pltpu.SMEM(occ_sym.shape, jnp.int32),
            pltpu.SMEM(vir_sym.shape, jnp.int32),
            pltpu.SMEM(k_sym.shape, jnp.int32),
            pltpu.VMEM((part, occ_rows), bf16),
            pltpu.VMEM((depth, columns), bf16),
            pltpu.VMEM((2, NX, NY, part, MAXO * BLK), bf16),
            pltpu.VMEM((NZ * depth, width), bf16),
            pltpu.VMEM((occ_rows, NZ * depth), bf16),
            pltpu.VMEM((MAXO * BLK, MAXO * BLK), bf16),
            dma((4 + PIECES,)),
            dma((2, v_count)), dma((2, v_count)),
            dma((3,)), dma((3,)),
            dma((2, 4)), dma((2, 4)),
            dma((NX,)), dma((NX,)),
        ],
        compiler_params=pltpu.CompilerParams(collective_id=0, has_side_effects=True, vmem_limit_bytes=24 << 20),
        name="ladder_ring",
    )(occ_sym, vir_sym, k_sym, in_hbm(amplitudes.T), in_hbm(integrals))
    return pl.pallas_call(
        expand_kernel,
        out_shape=jax.ShapeDtypeStruct((occ_rows, columns), bf16),
        in_specs=[vmem, vmem, vmem, smem, smem],
        out_specs=hbm,
        scratch_shapes=[
            pltpu.VMEM((occ_rows // BLK, BLK, width), bf16),
            pltpu.VMEM((occ_rows, columns), bf16),
            dma((2 + occ_rows // BLK,)),
        ],
        compiler_params=pltpu.CompilerParams(vmem_limit_bytes=24 << 20),
        name="expand",
    )(*parts)


def solution(mesh):
    return jax.shard_map(
        per_device,
        mesh=mesh,
        in_specs=(P("occ", "vir"), P("occ", "vir"), P("occ"), P("vir"), P()),
        out_specs=P("occ", "vir"),
        check_vma=False,
    )
```

```python
import jax
import jax.numpy as jnp
from jax import lax
from jax.experimental import pallas as pl
from jax.experimental.pallas import tpu as pltpu
from jax.sharding import PartitionSpec as P

BLK = 128
MAXO = 2
MAXB = 5
NZ, NY, NX = 8, 8, 4
PIECES = 4
FIRST_ORDER = "v1vv2v3vv4vxvvvcbbbvbbvbbb"
ORDER = "v1vv2v3vv4vvxvvvvcbbbbbbbb"
MESH = pl.DeviceIdType.MESH


def ladder_kernel(occ_hbm, vir_hbm, k_hbm, a_hbm, v_hbm, acc, a_last, v_last, occ_out, vir_out, occ_s, vir_s, k_s, a_in, v_in, ag, vbuf, amask, unit,
                  in_sem, vsend, vrecv, xsend, xrecv, ysend, yrecv, csend, crecv):
    occ_rows = acc.shape[0]
    occ_blocks = occ_rows // BLK
    depth = v_hbm.shape[0]
    vir_blocks = vir_s.shape[0]
    z = lax.axis_index("occ")
    v = lax.axis_index("vir")
    y = lax.div(v, 2 * NX)
    x = lax.rem(lax.div(v, 2), NX)
    c = lax.rem(v, 2)

    def vir_at(yy, xx, cc):
        return (yy * NX + xx) * 2 + cc

    def ring(value, step, size):
        return lax.rem(value + step + size, size)

    z_next, z_prev = (ring(z, 1, NZ), v), (ring(z, -1, NZ), v)
    y_next, y_prev = (z, vir_at(ring(y, 1, NY), x, c)), (z, vir_at(ring(y, -1, NY), x, c))
    x_far = {step: (z, vir_at(y, ring(x, step, NX), c)) for step in (1, 3, 2)}
    twin = (z, vir_at(y, x, 1 - c))
    partners = [z_next, z_prev, y_next, y_prev, twin] + list(x_far.values())

    rows = 2 * BLK // PIECES
    barrier = pltpu.get_barrier_semaphore()
    for partner in partners:
        pl.semaphore_signal(barrier, inc=1, device_id=partner, device_id_type=MESH)
    loads = [pltpu.make_async_copy(source, target, in_sem.at[index])
             for index, (source, target) in enumerate([(k_hbm, k_s), (vir_hbm, vir_s), (occ_hbm, occ_s), (a_hbm, a_in)])]
    v_loads = [pltpu.make_async_copy(v_hbm.at[piece * rows:(piece + 1) * rows], v_in.at[piece * rows:(piece + 1) * rows], in_sem.at[4 + piece])
               for piece in range(PIECES)]
    for load in loads:
        load.start()
    for piece in (0, 2, 1, 3):
        v_loads[piece].start()
    for load in loads[:3]:
        load.wait()

    def picks(labels, count, symmetry, slots):
        chosen, place = [], jnp.int32(1)
        for j in range(count):
            match = labels[j] == symmetry
            code = jnp.where(match, place, 0)
            chosen.append([code == 1 << t for t in range(slots)])
            place = jnp.where(match, 2 * place, place)
        return chosen

    def pick(blocks, chosen, t):
        value = blocks[t]
        for j in range(t + 1, len(blocks)):
            value = lax.select(chosen[j][t], blocks[j], value)
        return value

    own_picks = [picks(vir_s, vir_blocks, k_s[2 * z + half], MAXB) for half in range(2)]
    row_picks = picks(occ_s, occ_blocks, k_s[lax.div(v, 4)], MAXO)

    def pack(piece):
        v_loads[piece].wait()
        for strip in range(piece * rows, (piece + 1) * rows, 32):
            span = slice(strip, strip + 32)
            blocks = [v_in[span, j * BLK:(j + 1) * BLK] for j in range(vir_blocks)]
            for t in range(MAXB):
                vbuf[span, t * BLK:(t + 1) * BLK] = pick(blocks, own_picks[strip // BLK], t)

    pack(0)
    pack(2)
    pl.semaphore_wait(barrier, len(partners))

    piece_order = ((0, 1, 2, 3), (2, 3, 0, 1))
    slots = ((0, 1, 3, 5, 7), (0, 2, 4, 6, 7))

    def v_copy(way, index):
        step, piece = index // PIECES, piece_order[way][index % PIECES]
        source, target = [slots[way][step + ahead] * depth + piece * rows for ahead in range(2)]
        return pltpu.make_async_remote_copy(
            src_ref=vbuf.at[source:source + rows], dst_ref=vbuf.at[target:target + rows],
            send_sem=vsend.at[way, index], recv_sem=vrecv.at[way, index],
            device_id=(z_next, z_prev)[way], device_id_type=MESH)

    v_counts = (3 * PIECES + PIECES // 2, 4 * PIECES)
    v_copies = [[v_copy(way, index) for index in range(v_counts[way])] for way in range(2)]

    def y_copy(way, step):
        group = ring(y, -step if way == 0 else step, NY)
        return pltpu.make_async_remote_copy(
            src_ref=ag.at[c, x, group], dst_ref=ag.at[c, x, group], send_sem=ysend.at[way, step], recv_sem=yrecv.at[way, step],
            device_id=(y_next, y_prev)[way], device_id_type=MESH)

    def x_copy(step, group):
        part_of = ag.at[c, x] if group is None else ag.at[c, x, group]
        return pltpu.make_async_remote_copy(
            src_ref=part_of, dst_ref=part_of, send_sem=xsend.at[step - 1], recv_sem=xrecv.at[step - 1],
            device_id=x_far[step], device_id_type=MESH)

    def c_copy(step):
        column = ring(x, step, NX)
        return pltpu.make_async_remote_copy(
            src_ref=ag.at[c, column], dst_ref=ag.at[c, column], send_sem=csend.at[step], recv_sem=crecv.at[step],
            device_id=twin, device_id_type=MESH)

    y_copies = [[y_copy(0, step) for step in range(4)], [y_copy(1, step) for step in range(3)]]
    x_whole = [x_copy(step, None) for step in (1, 3, 2)]
    c_copies = [c_copy(step) for step in range(NX)]

    def x_send(step):
        group = ring(y, step, NY)
        for target in (1, 3, 2):
            x_copy(target, group).start()

    v_copies[0][0].start()
    v_copies[1][0].start()
    loads[3].wait()
    for t in range(MAXO):
        blocks = [a_in[:, i * BLK:(i + 1) * BLK] for i in range(occ_blocks)]
        ag[c, x, y, :, t * BLK:(t + 1) * BLK] = pick(blocks, row_picks, t)
    pack(1)
    pack(3)
    y_copies[0][0].start()
    y_copies[1][0].start()
    x_send(0)
    for index in range(1, PIECES):
        for way in range(2):
            v_copies[way][index].start()

    def when(holds, action):
        if holds is True:
            action()
        elif holds is not False:
            pl.when(holds)(action)

    def far(way, index, receiver):
        if index < 3 * PIECES:
            return True
        if way == 0:
            return receiver != 0
        return True if index < 3 * PIECES + PIECES // 2 else receiver == 0

    receivers = (ring(z, 1, NZ), ring(z, -1, NZ))

    def v_pass(index):
        for way in (1, 0):
            if index < len(v_copies[way]):
                when(far(way, index, z), v_copies[way][index].wait_recv)
            if index + PIECES < len(v_copies[way]):
                when(far(way, index + PIECES, receivers[way]), v_copies[way][index + PIECES].start)

    def y_pass(step):
        for way in range(2):
            if step <= len(y_copies[way]):
                y_copies[way][step - 1].wait_recv()
                if step < len(y_copies[way]):
                    y_copies[way][step].start()
                x_send(-step if way == 0 else step)
        if step == NY // 2:
            c_copies[0].start()

    ranks = []
    for i in range(occ_blocks):
        rank = jnp.int32(0)
        for other in range(i):
            rank = rank + jnp.where(occ_s[other] == occ_s[i], 1, 0)
        ranks.append(rank)

    def build(step):
        group = ring(y, -step, NY)
        distance = ring(z, -group, NZ)
        slot = 2 * jnp.minimum(distance, NZ - distance) - jnp.where((distance > 0) & (distance <= NZ // 2), 1, 0)
        nothing = jnp.zeros((BLK, BLK), jnp.bfloat16)
        for half in range(2):
            kb = group * 2 + half
            stacked = jnp.concatenate([ag[cc, 2 * half + xx, group] for xx in range(2) for cc in range(2)], axis=0)
            turned = lax.dot_general(unit[...], stacked, (((1,), (1,)), ((), ())), preferred_element_type=jnp.float32).astype(jnp.bfloat16)
            symmetry = k_s[kb]
            for i in range(occ_blocks):
                chosen = lax.select(ranks[i] == 0, turned[:BLK], turned[BLK:])
                amask[i * BLK:(i + 1) * BLK, pl.ds(pl.multiple_of(slot * depth + half * BLK, BLK), BLK)] = lax.select(occ_s[i] == symmetry, chosen, nothing)

    def product(first, last):
        return jnp.dot(amask[:, first * depth:last * depth], vbuf[first * depth:last * depth], preferred_element_type=jnp.float32)

    for i in range(occ_blocks):
        occ_out[i] = occ_s[i]
    for j in range(vir_blocks):
        vir_out[j] = vir_s[j]
    diagonal = [lax.broadcasted_iota(jnp.int32, unit.shape, axis) for axis in range(2)]
    unit[...] = (diagonal[0] == diagonal[1]).astype(jnp.bfloat16)
    def x_pass():
        for copy in x_whole:
            copy.wait_recv()
        for copy in c_copies[1:]:
            copy.start()

    def c_pass():
        for copy in c_copies:
            copy.wait_recv()

    def run(order):
        ring_steps, builds = iter(range(4 * PIECES)), iter((0, 1, 7, 2, 6, 3, 5, 4))
        for event in order:
            if event == "v":
                v_pass(next(ring_steps))
            elif event == "x":
                x_pass()
            elif event == "c":
                c_pass()
            elif event == "b":
                build(next(builds))
            else:
                y_pass(int(event))

    pl.when(z == 0)(lambda: run(FIRST_ORDER))
    pl.when(z != 0)(lambda: run(ORDER))
    a_last[...] = amask[:, 7 * depth:]
    acc[...] = product(0, 7)
    for index in range(3 * PIECES, 4 * PIECES):
        v_pass(index)
    v_last[...] = vbuf[7 * depth:]

    for way in range(2):
        for index, copy in enumerate(v_copies[way]):
            when(far(way, index, receivers[way]), copy.wait_send)
    for copy in x_whole + y_copies[0] + y_copies[1] + c_copies:
        copy.wait_send()


def expand_kernel(acc, a_last, v_last, occ_s, vir_s, out_hbm, packed, full, sems):
    copies = []
    for i in range(occ_s.shape[0]):
        span = slice(i * BLK, (i + 1) * BLK)
        rest = jnp.dot(a_last[span, :], v_last[...], preferred_element_type=jnp.float32)
        packed[i] = (acc[span, :] + rest).astype(packed.dtype)
        taken = jnp.int32(0)
        for j in range(vir_s.shape[0]):
            match = vir_s[j] == occ_s[i]
            slot = pl.multiple_of(jnp.minimum(taken, MAXB - 1) * BLK, BLK)
            block = packed[i, :, pl.ds(slot, BLK)]
            full[span, j * BLK:(j + 1) * BLK] = lax.select(match, block, jnp.zeros_like(block))
            taken = taken + jnp.where(match, 1, 0)
        copies.append(pltpu.make_async_copy(full.at[span], out_hbm.at[span], sems.at[2 + i]))
        copies[-1].start()
    for copy in copies:
        copy.wait()


def in_hbm(array):
    return pltpu.with_memory_space_constraint(array, pltpu.HBM)


def per_device(amplitudes, integrals, occ_sym, vir_sym, k_sym):
    occ_rows, part = amplitudes.shape
    depth, columns = integrals.shape
    width = MAXB * BLK
    bf16 = jnp.bfloat16
    vmem = pl.BlockSpec(memory_space=pltpu.VMEM)
    hbm = pl.BlockSpec(memory_space=pltpu.HBM)
    smem = pl.BlockSpec(memory_space=pltpu.SMEM)
    v_count = 4 * PIECES
    dma = pltpu.SemaphoreType.DMA
    occ_sym, vir_sym, k_sym = in_hbm(occ_sym), in_hbm(vir_sym), in_hbm(k_sym)
    parts = pl.pallas_call(
        ladder_kernel,
        out_shape=(pltpu.VMEM((occ_rows, width), jnp.float32), pltpu.VMEM((occ_rows, depth), bf16), pltpu.VMEM((depth, width), bf16), pltpu.SMEM(occ_sym.shape, jnp.int32), pltpu.SMEM(vir_sym.shape, jnp.int32)),
        in_specs=[hbm] * 5,
        out_specs=(vmem,) * 3 + (smem,) * 2,
        scratch_shapes=[
            pltpu.SMEM(occ_sym.shape, jnp.int32),
            pltpu.SMEM(vir_sym.shape, jnp.int32),
            pltpu.SMEM(k_sym.shape, jnp.int32),
            pltpu.VMEM((part, occ_rows), bf16),
            pltpu.VMEM((depth, columns), bf16),
            pltpu.VMEM((2, NX, NY, part, MAXO * BLK), bf16),
            pltpu.VMEM((NZ * depth, width), bf16),
            pltpu.VMEM((occ_rows, NZ * depth), bf16),
            pltpu.VMEM((MAXO * BLK, MAXO * BLK), bf16),
            dma((4 + PIECES,)),
            dma((2, v_count)), dma((2, v_count)),
            dma((3,)), dma((3,)),
            dma((2, 4)), dma((2, 4)),
            dma((NX,)), dma((NX,)),
        ],
        compiler_params=pltpu.CompilerParams(collective_id=0, has_side_effects=True, vmem_limit_bytes=24 << 20),
        name="ladder_ring",
    )(occ_sym, vir_sym, k_sym, in_hbm(amplitudes.T), in_hbm(integrals))
    return pl.pallas_call(
        expand_kernel,
        out_shape=jax.ShapeDtypeStruct((occ_rows, columns), bf16),
        in_specs=[vmem, vmem, vmem, smem, smem],
        out_specs=hbm,
        scratch_shapes=[
            pltpu.VMEM((occ_rows // BLK, BLK, width), bf16),
            pltpu.VMEM((occ_rows, columns), bf16),
            dma((2 + occ_rows // BLK,)),
        ],
        compiler_params=pltpu.CompilerParams(vmem_limit_bytes=24 << 20),
        name="expand",
    )(*parts)


def solution(mesh):
    return jax.shard_map(
        per_device,
        mesh=mesh,
        in_specs=(P("occ", "vir"), P("occ", "vir"), P("occ"), P("vir"), P()),
        out_specs=P("occ", "vir"),
        check_vma=False,
    )
```
